32 devices in a mesh: view: 8 (over z, core), strip: 2 (over x), orbit: 2 (over y).
Axes of the slice: x: 2, y: 2, z: 4, core: 2. Of those that a mesh axis runs over, the one named last changes fastest.
Arguments:
- features: bfloat16 [16, 8, 128, 256], P(('orbit', 'view'), 'strip'), parts along dimension 0, may hold values from -6 to 6
- cotangent: bfloat16 [16, 8, 128, 256], P(('orbit', 'view'), 'strip'), parts along dimension 0, may hold values from -6 to 6
- conv_first: bfloat16 [3, 3, 256, 256], replicated, may hold values from -0.125 to 0.125
- conv_second: bfloat16 [3, 3, 256, 256], replicated, may hold values from -0.125 to 0.125
- w_query: bfloat16 [256, 256], replicated, may hold values from -6 to 6
- w_key: bfloat16 [256, 256], replicated, may hold values from -6 to 6
- w_value: bfloat16 [256, 256], replicated, may hold values from -0.375 to 0.375
- w_out: bfloat16 [256, 256], replicated, may hold values from -0.375 to 0.375
Outputs:
- grad_features: bfloat16 [16, 8, 128, 256], P(('orbit', 'view'), 'strip'), parts along dimension 0
- conv_grads: float32 [4, 2304, 256], P('orbit', 'view'), parts along dimension 0
- attn_grads: float32 [8, 256, 256], P('orbit', 'view'), parts along dimension 0
The draws below stay inside these ranges and needn't reach their ends.
There are 2 independent parts, one for each index of `orbit`. The reference program is written for one: setup_inputs(seed, part) draws one part's arguments, and reference() takes and returns one part's arrays. A program takes and returns all parts, laid end to end along the dimension named above; an argument that names none is the same for every part. Nothing has to cross between parts.
All inputs are finite; a program needn't handle non-finite values.
Results may differ from the reference program's by a relative error of at most 0.017.
Values may be sent and summed in bfloat16 or wider, within the bound.
A program may use at most 64 MiB of HBM per device.

```python
import jax
import jax.numpy as jnp
from jax import lax

C = 256
COLS = 128
ROWS = 8
VIEWS = 8


def attention_pair(key):
    base = jax.random.fold_in(key, 4242)
    keys = jax.random.split(base, 3)
    scale = C ** (-0.5)
    noise_query = jnp.clip(jax.random.normal(keys[1], (C, C), jnp.float32), -6.0, 6.0)
    noise_key = jnp.clip(jax.random.normal(keys[2], (C, C), jnp.float32), -6.0, 6.0)
    first = scale * noise_query
    second = scale * noise_key
    return (first, second)


def draw_w_query(key, part):
    return attention_pair(key)[0].astype(jnp.bfloat16)


def draw_w_key(key, part):
    return attention_pair(key)[1].astype(jnp.bfloat16)


def shard_levels(stream_key, dims, cuts, least, top_value):
    loudness, own = 1.0, jax.random.fold_in(stream_key, 6)
    for dim, blocks in cuts:
        steps = jnp.exp(jax.random.uniform(jax.random.fold_in(own, dim), (blocks,), jnp.float32, least / len(cuts), top_value / len(cuts)))
        loudness = loudness * jnp.repeat(steps, dims[dim] // blocks).reshape([-1 if axis == dim else 1 for axis in range(len(dims))])
    return loudness


def bell_draw(key, shape, scale, bound, cuts=(), dtype=jnp.bfloat16):
    drawn = jax.random.normal(key, shape, jnp.float32) * scale
    if len(cuts) > 0:
        drawn = shard_levels(key, shape, cuts, -0.22, 0.18) * drawn
    return jnp.clip(drawn, min=-bound, max=bound).astype(dtype)


def setup_inputs(seed: int = 0, part: int = 0) -> dict:
    arg_keys = jax.random.split(jax.random.key(seed), 9)
    part_keys = jax.random.split(jax.random.fold_in(arg_keys[8], part), 9)
    return {
        "features": bell_draw(part_keys[0], (VIEWS, ROWS, COLS, C), 1.0, 6.0, ((0, 8), (1, 2))),
        "cotangent": bell_draw(part_keys[1], (VIEWS, ROWS, COLS, C), 1.0, 6.0, ((0, 8), (1, 2))),
        "conv_first": bell_draw(arg_keys[2], (3, 3, C, C), (9 * C) ** -0.5, 0.125),
        "conv_second": bell_draw(arg_keys[3], (3, 3, C, C), (9 * C) ** -0.5, 0.125),
        "w_query": draw_w_query(jax.random.fold_in(arg_keys[8], 71), part),
        "w_key": draw_w_key(jax.random.fold_in(arg_keys[8], 71), part),
        "w_value": bell_draw(arg_keys[6], (C, C), C ** -0.5, 0.375),
        "w_out": bell_draw(arg_keys[7], (C, C), C ** -0.5, 0.375),
    }


def rounded(array):
    return lax.optimization_barrier(array.astype(jnp.bfloat16))

def silu_slope(value):
    sigma = jax.nn.sigmoid(value)
    return sigma * (1.0 + value * (1.0 - sigma))

def pad_cells(array):
    return jnp.pad(array, ((0, 0), (1, 1), (1, 1), (0, 0)))

def flipped(kernel):
    return jnp.transpose(kernel[::-1, ::-1], (0, 1, 3, 2))

def convolve(padded, kernel):
    lead = padded.shape[0]
    rows = padded.shape[1] - 2
    cols = padded.shape[2] - 2
    chan = padded.shape[3]
    total = jnp.zeros((lead * rows * cols, kernel.shape[3]), jnp.float32)
    for shift_row in range(3):
        for shift_col in range(3):
            piece = padded[:, shift_row:shift_row + rows, shift_col:shift_col + cols, :].reshape(-1, chan)
            total = total + jnp.dot(piece.astype(jnp.float32), kernel[shift_row, shift_col].astype(jnp.float32))
    return total.reshape(lead, rows, cols, -1)

def kernel_grad(padded, upstream):
    rows = padded.shape[1] - 2
    cols = padded.shape[2] - 2
    chan = padded.shape[3]
    flat_up = upstream.reshape(-1, upstream.shape[3]).astype(jnp.float32)
    pieces = []
    for shift_row in range(3):
        for shift_col in range(3):
            piece = padded[:, shift_row:shift_row + rows, shift_col:shift_col + cols, :].reshape(-1, chan)
            pieces.append(lax.dot_general(piece.astype(jnp.float32), flat_up, (((0,), (0,)), ((), ()))))
    return jnp.stack(pieces).reshape(9 * chan, -1)

def attend(query, key, value, grad_mixed):
    chan = query.shape[-1]
    scale = chan ** (-0.5)
    query_f = query.astype(jnp.float32)
    key_f = key.astype(jnp.float32)
    value_f = value.astype(jnp.float32)
    grad_f = grad_mixed.astype(jnp.float32)
    scores = jnp.einsum('amc,bmc->mab', query_f, key_f) * scale
    top = lax.optimization_barrier(jnp.max(scores, axis=-1, keepdims=True))
    expo = jnp.exp(scores - top)
    prob_f = expo / lax.optimization_barrier(jnp.sum(expo, axis=-1, keepdims=True))
    prob = rounded(prob_f).astype(jnp.float32)
    mixed = rounded(jnp.einsum('mab,bmc->amc', prob, value_f))
    grad_prob = jnp.einsum('amc,bmc->mab', grad_f, value_f)
    grad_value = rounded(jnp.einsum('mab,amc->bmc', prob, grad_f))
    inner = lax.optimization_barrier(jnp.sum(prob_f * grad_prob, axis=-1, keepdims=True))
    grad_score = rounded(prob_f * (grad_prob - inner) * scale).astype(jnp.float32)
    grad_query = rounded(jnp.einsum('mab,bmc->amc', grad_score, key_f))
    grad_key = rounded(jnp.einsum('mab,amc->bmc', grad_score, query_f))
    return (mixed, grad_query, grad_key, grad_value)

def project(flat, weight):
    return rounded(jnp.dot(flat.astype(jnp.float32), weight.astype(jnp.float32)))

def reference(features, cotangent, conv_first, conv_second, w_query, w_key, w_value, w_out):
    views = features.shape[0]
    chan = features.shape[3]
    inputs_f = features.astype(jnp.float32)
    act_first = rounded(jax.nn.silu(inputs_f))
    pad_first = pad_cells(act_first)
    hidden_first = rounded(convolve(pad_first, conv_first))
    act_second = rounded(jax.nn.silu(hidden_first.astype(jnp.float32)))
    pad_second = pad_cells(act_second)
    summed = rounded(inputs_f + convolve(pad_second, conv_second))
    summed_f = summed.astype(jnp.float32)
    centred = summed_f - lax.optimization_barrier(jnp.mean(summed_f, axis=-1, keepdims=True))
    inv_scale = lax.rsqrt(lax.optimization_barrier(jnp.mean(centred * centred, axis=-1, keepdims=True)) + 1e-05)
    normed_f = centred * inv_scale
    normed = rounded(normed_f)
    flat_normed = normed.reshape(-1, chan)
    flat_cot = cotangent.reshape(-1, chan)
    query = project(flat_normed, w_query)
    key = project(flat_normed, w_key)
    value = project(flat_normed, w_value)
    grad_mixed = project(flat_cot, jnp.transpose(w_out))
    shaped = lambda array: array.reshape(views, -1, chan)
    mixed, grad_query, grad_key, grad_value = attend(shaped(query), shaped(key), shaped(value), shaped(grad_mixed))
    mixed = mixed.reshape(-1, chan).astype(jnp.float32)
    grad_query = grad_query.reshape(-1, chan).astype(jnp.float32)
    grad_key = grad_key.reshape(-1, chan).astype(jnp.float32)
    grad_value = grad_value.reshape(-1, chan).astype(jnp.float32)
    normed_ff = flat_normed.astype(jnp.float32)
    contract = (((0,), (0,)), ((), ()))
    attn_grads = jnp.stack([lax.dot_general(normed_ff, grad_query, contract), lax.dot_general(normed_ff, grad_key, contract), lax.dot_general(normed_ff, grad_value, contract), lax.dot_general(mixed, flat_cot.astype(jnp.float32), contract)])
    back = jnp.dot(grad_query, jnp.transpose(w_query).astype(jnp.float32))
    back = back + jnp.dot(grad_key, jnp.transpose(w_key).astype(jnp.float32))
    back = back + jnp.dot(grad_value, jnp.transpose(w_value).astype(jnp.float32))
    grad_normed = rounded(back).astype(jnp.float32).reshape(features.shape)
    grad_summed = cotangent.astype(jnp.float32) + inv_scale * (grad_normed - lax.optimization_barrier(jnp.mean(grad_normed, axis=-1, keepdims=True)) - normed_f * lax.optimization_barrier(jnp.mean(grad_normed * normed_f, axis=-1, keepdims=True)))
    grad_second = rounded(grad_summed)
    slope_second = convolve(pad_cells(grad_second), flipped(conv_second))
    grad_first = rounded(slope_second * silu_slope(hidden_first.astype(jnp.float32)))
    slope_first = convolve(pad_cells(grad_first), flipped(conv_first))
    grad_features = (grad_summed + slope_first * silu_slope(inputs_f)).astype(jnp.bfloat16)
    conv_grads = jnp.stack([kernel_grad(pad_first, grad_first), kernel_grad(pad_second, grad_second)])
    return (grad_features, conv_grads, attn_grads)
```

```python
import functools

import jax
import jax.numpy as jnp
from jax import lax
from jax.experimental import pallas as pl
from jax.experimental.pallas import tpu as pltpu
from jax.sharding import PartitionSpec as P

MESH = pl.DeviceIdType.MESH
F32 = jnp.float32
BF16 = jnp.bfloat16
NT = (((1,), (1,)), ((), ()))
TN = (((0,), (0,)), ((), ()))


def dot(a, b):
    return jnp.dot(a, b, preferred_element_type=F32)


def dot_nt(a, b):
    return lax.dot_general(a, b, NT, preferred_element_type=F32)


def dot_tn(a, b):
    return lax.dot_general(a, b, TN, preferred_element_type=F32)


def silu(x):
    return x * jax.nn.sigmoid(x)


def silu_slope(x):
    sigma = jax.nn.sigmoid(x)
    return sigma * (1.0 + x * (1.0 - sigma))


def kernel(
    dims, feat, cot, w1, w2, wq, wk, wv, wo, gfeat, conv_out, attn_out,
    cols1, cols2, colsg, halo, hidden, act2, normed, normed_f, inv, g2, g1, gs,
    normp, cotp, backp, gn,
    part_a, part_b, part_c, r1a, r1b, r1c, sum_a, sum_b, sum_c,
    r2a, r2b, r2c, r3a, r3b, r3c,
    halo_send, halo_recv, cot_send, cot_recv, nrm_send, nrm_recv, bck_send, bck_recv,
    s1_send, s1_recv, s2_send, s2_recv, s3_send, s3_recv,
):
    views, strips, rows, width, chan = dims
    pixels = rows * width
    share = pixels // views
    zs = views // 2
    view = lax.axis_index("view")
    strip = lax.axis_index("strip")
    core = lax.rem(view, 2)
    zed = lax.div(view, 2)

    barrier = pltpu.get_barrier_semaphore()
    for k in range(1, views):
        pl.semaphore_signal(
            barrier, inc=1, device_id={"view": lax.rem(view + k, views)}, device_id_type=MESH
        )
    for k in range(1, strips):
        pl.semaphore_signal(
            barrier, inc=1, device_id={"strip": lax.rem(strip + k, strips)}, device_id_type=MESH
        )

    @pl.when(strip == 0)
    def _():
        for e in range(4):
            halo[e, 0] = jnp.zeros((width, chan), BF16)

    @pl.when(strip == strips - 1)
    def _():
        for e in range(4):
            halo[e, 1] = jnp.zeros((width, chan), BF16)

    pl.semaphore_wait(barrier, views - 1 + strips - 1)

    def halo_copies(e, ref):
        up = pltpu.make_async_remote_copy(
            src_ref=ref.at[pl.ds(0, width)], dst_ref=halo.at[e, 1],
            send_sem=halo_send.at[e, 0], recv_sem=halo_recv.at[e, 0],
            device_id={"strip": lax.max(strip - 1, 0)}, device_id_type=MESH,
        )
        down = pltpu.make_async_remote_copy(
            src_ref=ref.at[pl.ds(pixels - width, width)], dst_ref=halo.at[e, 0],
            send_sem=halo_send.at[e, 1], recv_sem=halo_recv.at[e, 1],
            device_id={"strip": lax.min(strip + 1, strips - 1)}, device_id_type=MESH,
        )
        return up, down

    def halo_start(e, ref):
        up, down = halo_copies(e, ref)
        pl.when(strip > 0)(up.start)
        pl.when(strip < strips - 1)(down.start)

    def halo_wait(e, ref):
        up, down = halo_copies(e, ref)

        @pl.when(strip > 0)
        def _():
            up.wait_send()
            down.wait_recv()

        @pl.when(strip < strips - 1)
        def _():
            down.wait_send()
            up.wait_recv()

    def spread(src, dst, send, recv):
        out = []
        for k in range(1, views):
            peer = lax.rem(view + k, views)
            out.append(
                pltpu.make_async_remote_copy(
                    src_ref=src.at[pl.ds(pl.multiple_of(peer * share, share), share)],
                    dst_ref=dst.at[pl.ds(pl.multiple_of(view * share, share), share)],
                    send_sem=send.at[k], recv_sem=recv.at[k],
                    device_id={"view": peer}, device_id_type=MESH,
                )
            )
        return out

    mine = pl.ds(pl.multiple_of(view * share, share), share)

    def start(copies):
        for copy in copies:
            copy.start()

    def wait(copies):
        for copy in copies:
            copy.wait()

    column = lax.rem(lax.broadcasted_iota(jnp.int32, (pixels + 2 * width, chan), 0), width)

    def build(cols, e, centre, act):
        top = act(halo[e, 0].astype(F32))
        low = act(halo[e, 1].astype(F32))
        x = jnp.concatenate([top, centre, low], axis=0)
        count = pixels + 2 * width
        left = jnp.where(column == 0, 0.0, pltpu.roll(x, 1, 0))
        right = jnp.where(column == width - 1, 0.0, pltpu.roll(x, count - 1, 0))
        cols[:, pl.ds(0, chan)] = left.astype(BF16)
        cols[:, pl.ds(chan, chan)] = x.astype(BF16)
        cols[:, pl.ds(2 * chan, chan)] = right.astype(BF16)

    def conv(cols, w):
        total = None
        for r in range(3):
            term = dot(cols[pl.ds(r * width, pixels), :], w[r])
            total = term if total is None else total + term
        return total

    def conv_flip(cols, w):
        total = None
        for r in range(3):
            for s in range(3):
                term = dot_nt(
                    cols[pl.ds(r * width, pixels), pl.ds(s * chan, chan)],
                    w[2 - r, pl.ds((2 - s) * chan, chan), :],
                )
                total = term if total is None else total + term
        return total

    def wgrad(cols, d, out):
        for r in range(3):
            value = dot_tn(cols[pl.ds(r * width, pixels), :], d).astype(BF16)
            flat = out.reshape(9 * chan, chan)
            flat[pl.ds(r * 3 * chan, 3 * chan), :] = value

    def same(x):
        return x

    def stage1(i, part, r1):
        return pltpu.make_async_remote_copy(
            src_ref=part.at[:, 1 - core], dst_ref=r1,
            send_sem=s1_send.at[i], recv_sem=s1_recv.at[i],
            device_id={"view": view + 1 - 2 * core}, device_id_type=MESH,
        )

    def reduce1(part, r1, total):
        for j in range(zs):
            total[j] = (part[j, core].astype(F32) + r1[j].astype(F32)).astype(BF16)

    def stage2(i, total, r2):
        out = []
        for k in range(1, zs):
            other = lax.rem(zed + k, zs)
            out.append(
                pltpu.make_async_remote_copy(
                    src_ref=total.at[other], dst_ref=r2.at[k - 1],
                    send_sem=s2_send.at[i, k], recv_sem=s2_recv.at[i, k],
                    device_id={"view": other * 2 + core}, device_id_type=MESH,
                )
            )
        return out

    def reduce2(total, r2, r3):
        value = total[zed].astype(F32)
        for k in range(1, zs):
            value = value + r2[k - 1].astype(F32)
        r3[strip] = value.astype(BF16)

    def stage3(i, r3):
        out = []
        for k in range(1, strips):
            out.append(
                pltpu.make_async_remote_copy(
                    src_ref=r3.at[strip], dst_ref=r3.at[strip],
                    send_sem=s3_send.at[i, k], recv_sem=s3_recv.at[i, k],
                    device_id={"strip": lax.rem(strip + k, strips)}, device_id_type=MESH,
                )
            )
        return out

    def reduce3(r3):
        value = r3[0].astype(F32)
        for k in range(1, strips):
            value = value + r3[k].astype(F32)
        return value

    halo_start(0, feat)
    cot_copies = spread(cot, cotp, cot_send, cot_recv)
    start(cot_copies)
    cotp[mine, :] = cot[mine, :]
    x = feat[...].astype(F32)
    a1 = silu(x)
    halo_wait(0, feat)
    build(cols1, 0, a1, silu)
    hidden[...] = conv(cols1, w1).astype(BF16)
    act2[...] = silu(hidden[...].astype(F32)).astype(BF16)
    halo_start(1, act2)
    halo_wait(1, act2)
    build(cols2, 1, act2[...].astype(F32), same)
    summed = (feat[...].astype(F32) + conv(cols2, w2)).astype(BF16).astype(F32)
    centred = summed - jnp.mean(summed, axis=-1, keepdims=True)
    scale = lax.rsqrt(jnp.mean(centred * centred, axis=-1, keepdims=True) + 1e-05)
    inv[...] = jnp.broadcast_to(scale, inv.shape)
    nf = centred * scale
    normed_f[...] = nf
    normed[...] = nf.astype(BF16)
    nrm_copies = spread(normed, normp, nrm_send, nrm_recv)
    start(nrm_copies)
    normp[mine, :] = normed[mine, :]
    wait(cot_copies)
    gmix = dot_nt(cotp[...], wo[...]).astype(BF16)
    wait(nrm_copies)

    rp = normp[...]
    query = dot(rp, wq[...]).astype(BF16)
    key = dot(rp, wk[...]).astype(BF16)
    value = dot(rp, wv[...]).astype(BF16)
    n = views * share
    ia = lax.rem(lax.broadcasted_iota(jnp.int32, (n, n), 0), share)
    ib = lax.rem(lax.broadcasted_iota(jnp.int32, (n, n), 1), share)
    factor = chan ** (-0.5)
    scores = jnp.where(ia == ib, dot_nt(query, key) * factor, -jnp.inf)
    expo = jnp.exp(scores - jnp.max(scores, axis=-1, keepdims=True))
    prob_f = expo / jnp.sum(expo, axis=-1, keepdims=True)
    prob = prob_f.astype(BF16)
    mixed = dot(prob, value).astype(BF16)
    grad_prob = dot_nt(gmix, value)
    weighted = prob_f * grad_prob
    inner = jnp.sum(weighted, axis=-1, keepdims=True)
    grad_score = (prob_f * (grad_prob - inner) * factor).astype(BF16)
    grad_value = dot_tn(prob, gmix).astype(BF16)
    grad_query = dot(grad_score, key).astype(BF16)
    grad_key = dot_tn(grad_score, query).astype(BF16)
    back = dot_nt(grad_query, wq[...]) + dot_nt(grad_key, wk[...]) + dot_nt(grad_value, wv[...])
    backp[...] = back.astype(BF16)
    bck_copies = spread(backp, gn, bck_send, bck_recv)
    start(bck_copies)
    gn[mine, :] = backp[mine, :]
    slab = chan // views
    for t, (lhs, rhs) in enumerate(
        ((rp, grad_query), (rp, grad_key), (rp, grad_value), (mixed, cotp[...]))
    ):
        term = dot_tn(lhs, rhs).astype(BF16)
        part_a[:, :, t] = term.reshape(zs, 2, slab, chan)
    a1_copy = stage1(0, part_a, r1a)
    a1_copy.start()

    wait(bck_copies)
    gnf = gn[...].astype(F32)
    nf = normed_f[...]
    gsum = cot[...].astype(F32) + inv[:, 0:1] * (
        gnf
        - jnp.mean(gnf, axis=-1, keepdims=True)
        - nf * jnp.mean(gnf * nf, axis=-1, keepdims=True)
    )
    gs[...] = gsum
    g2[...] = gsum.astype(BF16)
    halo_start(2, g2)
    wgrad(cols2, g2[...], part_b)
    b1_copy = stage1(1, part_b, r1b)
    b1_copy.start()
    a1_copy.wait()
    reduce1(part_a, r1a, sum_a)
    a2_copies = stage2(0, sum_a, r2a)
    start(a2_copies)
    halo_wait(2, g2)
    build(colsg, 2, g2[...].astype(F32), same)
    slope = conv_flip(colsg, w2)
    g1[...] = (slope * silu_slope(hidden[...].astype(F32))).astype(BF16)
    halo_start(3, g1)
    b1_copy.wait()
    reduce1(part_b, r1b, sum_b)
    b2_copies = stage2(1, sum_b, r2b)
    start(b2_copies)
    wgrad(cols1, g1[...], part_c)
    c1_copy = stage1(2, part_c, r1c)
    c1_copy.start()
    halo_wait(3, g1)
    build(colsg, 3, g1[...].astype(F32), same)
    c1_copy.wait()
    reduce1(part_c, r1c, sum_c)
    c2_copies = stage2(2, sum_c, r2c)
    start(c2_copies)
    slope = conv_flip(colsg, w1)
    gfeat[...] = (gs[...] + slope * silu_slope(feat[...].astype(F32))).astype(BF16)
    wait(a2_copies)
    reduce2(sum_a, r2a, r3a)
    a3_copies = stage3(0, r3a)
    start(a3_copies)
    wait(b2_copies)
    reduce2(sum_b, r2b, r3b)
    b3_copies = stage3(1, r3b)
    start(b3_copies)
    wait(a3_copies)
    attn_out[...] = reduce3(r3a)
    wait(b3_copies)
    conv_out[1] = reduce3(r3b)
    wait(c2_copies)
    reduce2(sum_c, r2c, r3c)
    c3_copies = stage3(2, r3c)
    start(c3_copies)
    wait(c3_copies)
    conv_out[0] = reduce3(r3c)


def body(features, cotangent, conv_first, conv_second, w_query, w_key, w_value, w_out):
    views = lax.axis_size("view")
    strips = lax.axis_size("strip")
    _, rows, width, chan = features.shape
    pixels = rows * width
    zs = views // 2
    cut = 9 * chan // views
    slab = chan // views
    vm = pltpu.VMEM
    dma = pltpu.SemaphoreType.DMA
    padded = pixels + 2 * width
    flat = (pixels, chan)
    conv_s = (cut, chan)
    attn_s = (4, slab, chan)
    scratch = [
        vm((padded, 3 * chan), BF16), vm((padded, 3 * chan), BF16), vm((padded, 3 * chan), BF16),
        vm((4, 2, width, chan), BF16),
        vm(flat, BF16), vm(flat, BF16), vm(flat, BF16), vm(flat, F32), vm((pixels, 128), F32),
        vm(flat, BF16), vm(flat, BF16), vm(flat, F32),
        vm(flat, BF16), vm(flat, BF16), vm(flat, BF16), vm(flat, BF16),
        vm((zs, 2) + attn_s, BF16), vm((zs, 2) + conv_s, BF16), vm((zs, 2) + conv_s, BF16),
        vm((zs,) + attn_s, BF16), vm((zs,) + conv_s, BF16), vm((zs,) + conv_s, BF16),
        vm((zs,) + attn_s, BF16), vm((zs,) + conv_s, BF16), vm((zs,) + conv_s, BF16),
        vm((zs - 1,) + attn_s, BF16), vm((zs - 1,) + conv_s, BF16), vm((zs - 1,) + conv_s, BF16),
        vm((strips,) + attn_s, BF16), vm((strips,) + conv_s, BF16), vm((strips,) + conv_s, BF16),
        dma((4, 2)), dma((4, 2)),
        dma((views,)), dma((views,)), dma((views,)), dma((views,)), dma((views,)), dma((views,)),
        dma((3,)), dma((3,)), dma((3, zs)), dma((3, zs)), dma((3, strips)), dma((3, strips)),
    ]
    spec = pl.BlockSpec(memory_space=pltpu.VMEM)
    outs = pl.pallas_call(
        functools.partial(kernel, (views, strips, rows, width, chan)),
        out_shape=(
            jax.ShapeDtypeStruct(flat, BF16),
            jax.ShapeDtypeStruct((2,) + conv_s, F32),
            jax.ShapeDtypeStruct(attn_s, F32),
        ),
        in_specs=[spec] * 8,
        out_specs=(spec, spec, spec),
        scratch_shapes=scratch,
        compiler_params=pltpu.CompilerParams(
            collective_id=0, has_side_effects=True, vmem_limit_bytes=60 * 1024 * 1024
        ),
    )(
        features.reshape(flat),
        cotangent.reshape(flat),
        conv_first.reshape(3, 3 * chan, chan),
        conv_second.reshape(3, 3 * chan, chan),
        w_query, w_key, w_value, w_out,
    )
    return (outs[0].reshape(features.shape), outs[1], outs[2])


def solution(mesh):
    rows = P(("orbit", "view"), "strip", None, None)
    grads = P("orbit", "view", None)
    return jax.shard_map(
        body,
        mesh=mesh,
        in_specs=(rows, rows, P(), P(), P(), P(), P(), P()),
        out_specs=(rows, grads, grads),
        check_vma=False,
    )
```

```python
import functools

import jax
import jax.numpy as jnp
from jax import lax
from jax.experimental import pallas as pl
from jax.experimental.pallas import tpu as pltpu
from jax.sharding import PartitionSpec as P

MESH = pl.DeviceIdType.MESH
F32 = jnp.float32
BF16 = jnp.bfloat16
NT = (((1,), (1,)), ((), ()))
TN = (((0,), (0,)), ((), ()))


def dot(a, b):
    return jnp.dot(a, b, preferred_element_type=F32)


def dot_nt(a, b):
    return lax.dot_general(a, b, NT, preferred_element_type=F32)


def dot_tn(a, b):
    return lax.dot_general(a, b, TN, preferred_element_type=F32)


def silu(x):
    return x * jax.nn.sigmoid(x)


def silu_slope(x):
    sigma = jax.nn.sigmoid(x)
    return sigma * (1.0 + x * (1.0 - sigma))


def kernel(
    dims, feat, cot, w1h, w2h, wqh, wkh, wvh, woh, gfeat, conv_out, attn_out,
    w1, w2, wq, wk, wv, wo, load,
    cols1, cols2, colsg, halo, hidden, act2, normed, normed_f, inv, g2, g1, gs,
    normp, cotp, backp, gn,
    part_a, part_b, part_c, r1a, r1b, r1c, t1a, t1b, t1c, r2a, r2b, r2c,
    t2a, t2b, t2c, r3a, r3b, r3c, r4a, r4b, r4c,
    halo_send, halo_recv, cot_send, cot_recv, nrm_send, nrm_recv, bck_send, bck_recv,
    s1_send, s1_recv, s2_send, s2_recv, s3_send, s3_recv, s4_send, s4_recv,
):
    views, strips, rows, width, chan = dims
    pixels = rows * width
    share = pixels // views
    zs = views // 2
    view = lax.axis_index("view")
    strip = lax.axis_index("strip")
    core = lax.rem(view, 2)
    zed = lax.div(view, 2)

    loads = [
        pltpu.make_async_copy(src, dst, load.at[i])
        for i, (src, dst) in enumerate(
            ((w1h, w1), (w2h, w2), (woh, wo), (wqh, wq), (wkh, wk), (wvh, wv))
        )
    ]
    for item in loads:
        item.start()
    barrier = pltpu.get_barrier_semaphore()
    for k in range(1, views):
        pl.semaphore_signal(
            barrier, inc=1, device_id={"view": lax.rem(view + k, views)}, device_id_type=MESH
        )
    for k in range(1, strips):
        pl.semaphore_signal(
            barrier, inc=1, device_id={"strip": lax.rem(strip + k, strips)}, device_id_type=MESH
        )

    @pl.when(strip == 0)
    def _():
        for e in range(4):
            halo[e, 0] = jnp.zeros((width, chan), BF16)

    @pl.when(strip == strips - 1)
    def _():
        for e in range(4):
            halo[e, 1] = jnp.zeros((width, chan), BF16)

    pl.semaphore_wait(barrier, views - 1 + strips - 1)

    def halo_copies(e, ref):
        up = pltpu.make_async_remote_copy(
            src_ref=ref.at[pl.ds(0, width)], dst_ref=halo.at[e, 1],
            send_sem=halo_send.at[e, 0], recv_sem=halo_recv.at[e, 0],
            device_id={"strip": lax.max(strip - 1, 0)}, device_id_type=MESH,
        )
        down = pltpu.make_async_remote_copy(
            src_ref=ref.at[pl.ds(pixels - width, width)], dst_ref=halo.at[e, 0],
            send_sem=halo_send.at[e, 1], recv_sem=halo_recv.at[e, 1],
            device_id={"strip": lax.min(strip + 1, strips - 1)}, device_id_type=MESH,
        )
        return up, down

    def halo_start(e, ref):
        up, down = halo_copies(e, ref)
        pl.when(strip > 0)(up.start)
        pl.when(strip < strips - 1)(down.start)

    def halo_wait(e, ref):
        up, down = halo_copies(e, ref)

        @pl.when(strip > 0)
        def _():
            up.wait_send()
            down.wait_recv()

        @pl.when(strip < strips - 1)
        def _():
            down.wait_send()
            up.wait_recv()

    def spread(src, dst, send, recv):
        out = []
        for k in range(1, views):
            peer = lax.rem(view + k, views)
            out.append(
                pltpu.make_async_remote_copy(
                    src_ref=src.at[pl.ds(pl.multiple_of(peer * share, share), share)],
                    dst_ref=dst.at[pl.ds(pl.multiple_of(view * share, share), share)],
                    send_sem=send.at[k], recv_sem=recv.at[k],
                    device_id={"view": peer}, device_id_type=MESH,
                )
            )
        return out

    mine = pl.ds(pl.multiple_of(view * share, share), share)

    def start(copies):
        for copy in copies:
            copy.start()

    def wait(copies):
        for copy in copies:
            copy.wait()

    column = lax.rem(lax.broadcasted_iota(jnp.int32, (pixels + 2 * width, chan), 0), width)

    def build(cols, e, centre, act):
        top = act(halo[e, 0].astype(F32))
        low = act(halo[e, 1].astype(F32))
        x = jnp.concatenate([top, centre, low], axis=0)
        count = pixels + 2 * width
        left = jnp.where(column == 0, 0.0, pltpu.roll(x, 1, 0))
        right = jnp.where(column == width - 1, 0.0, pltpu.roll(x, count - 1, 0))
        cols[:, pl.ds(0, chan)] = left.astype(BF16)
        cols[:, pl.ds(chan, chan)] = x.astype(BF16)
        cols[:, pl.ds(2 * chan, chan)] = right.astype(BF16)

    def conv(cols, w):
        total = None
        for r in range(3):
            term = dot(cols[pl.ds(r * width, pixels), :], w[r])
            total = term if total is None else total + term
        return total

    def conv_flip(cols, w):
        total = None
        for r in range(3):
            for s in range(3):
                term = dot_nt(
                    cols[pl.ds(r * width, pixels), pl.ds(s * chan, chan)],
                    w[2 - r, pl.ds((2 - s) * chan, chan), :],
                )
                total = term if total is None else total + term
        return total

    def wgrad(cols, d, out):
        pieces, _, _, parts, unit, _ = out.shape
        per = 3 * chan // unit
        for r in range(3):
            value = dot_tn(cols[pl.ds(r * width, pixels), :], d).astype(BF16)
            for m in range(per):
                u = r * per + m
                v, rest = divmod(u, pieces * parts)
                p, t = divmod(rest, parts)
                out[p, v // 2, v % 2, t] = value[m * unit : (m + 1) * unit]

    def same(x):
        return x

    def group(base, part, r1, t1, r2, t2, r3, r4):
        parts = part.shape[3]

        def stage1(p):
            return [
                pltpu.make_async_remote_copy(
                    src_ref=part.at[p, :, 1 - core], dst_ref=r1.at[p],
                    send_sem=s1_send.at[base + p], recv_sem=s1_recv.at[base + p],
                    device_id={"view": view + 1 - 2 * core}, device_id_type=MESH,
                )
            ]

        def reduce1(p):
            for j in range(zs):
                for t in range(parts):
                    t1[p, t, j] = (
                        part[p, j, core, t].astype(F32) + r1[p, j, t].astype(F32)
                    ).astype(BF16)

        def stage2(p):
            out = []
            for k in range(1, parts):
                other = lax.rem(strip + k, strips)
                out.append(
                    pltpu.make_async_remote_copy(
                        src_ref=t1.at[p, other], dst_ref=r2.at[p, k - 1],
                        send_sem=s2_send.at[base + p, k], recv_sem=s2_recv.at[base + p, k],
                        device_id={"strip": other}, device_id_type=MESH,
                    )
                )
            return out

        def reduce2(p):
            own = strip if parts > 1 else 0
            for j in range(zs):
                value = t1[p, own, j].astype(F32)
                for k in range(1, parts):
                    value = value + r2[p, k - 1, j].astype(F32)
                t2[p, j] = value.astype(BF16)

        def stage3(p):
            out = []
            for k in range(1, zs):
                other = lax.rem(zed + k, zs)
                out.append(
                    pltpu.make_async_remote_copy(
                        src_ref=t2.at[p, other], dst_ref=r3.at[p, k - 1],
                        send_sem=s3_send.at[base + p, k], recv_sem=s3_recv.at[base + p, k],
                        device_id={"view": other * 2 + core}, device_id_type=MESH,
                    )
                )
            return out

        def reduce3(p):
            value = t2[p, zed].astype(F32)
            for k in range(1, zs):
                value = value + r3[p, k - 1].astype(F32)
            r4[p, strip] = value.astype(BF16)

        def stage4(p):
            out = []
            for k in range(1, strips):
                out.append(
                    pltpu.make_async_remote_copy(
                        src_ref=r4.at[p, strip], dst_ref=r4.at[p, strip],
                        send_sem=s4_send.at[base + p, k], recv_sem=s4_recv.at[base + p, k],
                        device_id={"strip": lax.rem(strip + k, strips)}, device_id_type=MESH,
                    )
                )
            return out

        def final(p):
            if parts > 1:
                return [r4[p, t].astype(F32) for t in range(parts)]
            value = r4[p, 0].astype(F32)
            for t in range(1, strips):
                value = value + r4[p, t].astype(F32)
            return [value]

        reduces = (None, reduce1, reduce2, reduce3)
        stages = (stage1, stage2, stage3, stage4)

        def launch():
            for p in range(part.shape[0]):
                start(stage1(p))

        def advance(k, p):
            wait(stages[k - 1](p))
            reduces[k](p)
            start(stages[k](p))

        def advance_all(k):
            for p in range(part.shape[0]):
                advance(k, p)

        def finish(store):
            for p in range(part.shape[0]):
                wait(stage4(p))
                for t, value in enumerate(final(p)):
                    store(p * parts + t, value)

        return launch, advance_all, finish

    count_a = part_a.shape[0]
    count_b = part_b.shape[0]
    launch_a, step_a, finish_a = group(0, part_a, r1a, t1a, r2a, t2a, r3a, r4a)
    launch_b, step_b, finish_b = group(count_a, part_b, r1b, t1b, r2b, t2b, r3b, r4b)
    launch_c, step_c, finish_c = group(count_a + count_b, part_c, r1c, t1c, r2c, t2c, r3c, r4c)

    halo_start(0, feat)
    cot_copies = spread(cot, cotp, cot_send, cot_recv)
    start(cot_copies)
    cotp[mine, :] = cot[mine, :]
    x = feat[...].astype(F32)
    a1 = silu(x)
    halo_wait(0, feat)
    build(cols1, 0, a1, silu)
    loads[0].wait()
    hidden[...] = conv(cols1, w1).astype(BF16)
    act2[...] = silu(hidden[...].astype(F32)).astype(BF16)
    halo_start(1, act2)
    halo_wait(1, act2)
    build(cols2, 1, act2[...].astype(F32), same)
    loads[1].wait()
    summed = (feat[...].astype(F32) + conv(cols2, w2)).astype(BF16).astype(F32)
    centred = summed - jnp.mean(summed, axis=-1, keepdims=True)
    scale = lax.rsqrt(jnp.mean(centred * centred, axis=-1, keepdims=True) + 1e-05)
    inv[...] = jnp.broadcast_to(scale, inv.shape)
    nf = centred * scale
    normed_f[...] = nf
    normed[...] = nf.astype(BF16)
    nrm_copies = spread(normed, normp, nrm_send, nrm_recv)
    start(nrm_copies)
    normp[mine, :] = normed[mine, :]
    wait(cot_copies)
    loads[2].wait()
    gmix = dot_nt(cotp[...], wo[...]).astype(BF16)
    for item in loads[3:]:
        item.wait()
    wait(nrm_copies)

    rp = normp[...]
    query = dot(rp, wq[...]).astype(BF16)
    key = dot(rp, wk[...]).astype(BF16)
    value = dot(rp, wv[...]).astype(BF16)
    n = views * share
    ia = lax.rem(lax.broadcasted_iota(jnp.int32, (n, n), 0), share)
    ib = lax.rem(lax.broadcasted_iota(jnp.int32, (n, n), 1), share)
    factor = chan ** (-0.5)
    scores = jnp.where(ia == ib, dot_nt(query, key) * factor, -jnp.inf)
    expo = jnp.exp(scores - jnp.max(scores, axis=-1, keepdims=True))
    prob_f = expo / jnp.sum(expo, axis=-1, keepdims=True)
    prob = prob_f.astype(BF16)
    mixed = dot(prob, value).astype(BF16)
    grad_prob = dot_nt(gmix, value)
    weighted = prob_f * grad_prob
    inner = jnp.sum(weighted, axis=-1, keepdims=True)
    grad_score = (prob_f * (grad_prob - inner) * factor).astype(BF16)
    grad_value = dot_tn(prob, gmix).astype(BF16)
    grad_query = dot(grad_score, key).astype(BF16)
    grad_key = dot_tn(grad_score, query).astype(BF16)
    back = dot_nt(grad_query, wq[...]) + dot_nt(grad_key, wk[...]) + dot_nt(grad_value, wv[...])
    backp[...] = back.astype(BF16)
    bck_copies = spread(backp, gn, bck_send, bck_recv)
    start(bck_copies)
    gn[mine, :] = backp[mine, :]
    parts = part_a.shape[3]
    unit = chan // (views * parts)
    for t, (lhs, rhs) in enumerate(
        ((rp, grad_query), (rp, grad_key), (rp, grad_value), (mixed, cotp[...]))
    ):
        term = dot_tn(lhs, rhs).astype(BF16)
        for u in range(views * parts):
            v, q = divmod(u, parts)
            part_a[0, v // 2, v % 2, q, t] = term[u * unit : (u + 1) * unit]
    launch_a()
    step_a(1)

    wait(bck_copies)
    gnf = gn[...].astype(F32)
    nf = normed_f[...]
    gsum = cot[...].astype(F32) + inv[:, 0:1] * (
        gnf
        - jnp.mean(gnf, axis=-1, keepdims=True)
        - nf * jnp.mean(gnf * nf, axis=-1, keepdims=True)
    )
    gs[...] = gsum
    g2[...] = gsum.astype(BF16)
    halo_start(2, g2)
    wgrad(cols2, g2[...], part_b)
    launch_b()
    step_a(2)
    step_b(1)
    halo_wait(2, g2)
    build(colsg, 2, g2[...].astype(F32), same)
    slope = conv_flip(colsg, w2)
    g1[...] = (slope * silu_slope(hidden[...].astype(F32))).astype(BF16)
    halo_start(3, g1)
    wgrad(cols1, g1[...], part_c)
    launch_c()
    step_c(1)
    step_b(2)
    halo_wait(3, g1)
    build(colsg, 3, g1[...].astype(F32), same)
    slope = conv_flip(colsg, w1)
    gfeat[...] = (gs[...] + slope * silu_slope(feat[...].astype(F32))).astype(BF16)
    step_a(3)
    step_c(2)
    step_b(3)
    step_c(3)

    def store_a(u, value):
        attn_out[:, pl.ds(u * unit, unit), :] = value.astype(attn_out.dtype)

    def store_conv(i):
        def store(u, value):
            size = value.shape[0]
            conv_out[i, pl.ds(u * size, size), :] = value.astype(conv_out.dtype)

        return store

    finish_a(store_a)
    finish_b(store_conv(1))
    finish_c(store_conv(0))


def widen(a, b, c, x, y, z):
    x[...] = a[...]
    y[...] = b[...].astype(F32)
    z[...] = c[...].astype(F32)


def body(features, cotangent, conv_first, conv_second, w_query, w_key, w_value, w_out):
    views = lax.axis_size("view")
    strips = lax.axis_size("strip")
    _, rows, width, chan = features.shape
    pixels = rows * width
    zs = views // 2
    cut = 9 * chan // views
    slab = chan // views
    vm = pltpu.VMEM
    dma = pltpu.SemaphoreType.DMA
    padded = pixels + 2 * width
    flat = (pixels, chan)
    exact = cut % (16 * strips) == 0 and slab % (16 * strips) == 0
    parts = strips if exact else 1
    pieces = 3 if cut % (48 * parts) == 0 else 1
    conv_u = (cut // (parts * pieces), chan)
    attn_u = (4, slab // parts, chan)
    units = ((1, attn_u), (pieces, conv_u), (pieces, conv_u))
    total = 1 + 2 * pieces
    hold = [
        [(n, zs, 2, parts) + u for n, u in units],
        [(n, zs, parts) + u for n, u in units],
        [(n, parts, zs) + u for n, u in units],
        [(n, max(parts - 1, 1), zs) + u for n, u in units],
        [(n, zs) + u for n, u in units],
        [(n, zs - 1) + u for n, u in units],
        [(n, strips) + u for n, u in units],
    ]
    conv_k = (3, 3 * chan, chan)
    square = (chan, chan)
    scratch = [
        vm(conv_k, BF16), vm(conv_k, BF16),
        vm(square, BF16), vm(square, BF16), vm(square, BF16), vm(square, BF16), dma((6,)),
        vm((padded, 3 * chan), BF16), vm((padded, 3 * chan), BF16), vm((padded, 3 * chan), BF16),
        vm((4, 2, width, chan), BF16),
        vm(flat, BF16), vm(flat, BF16), vm(flat, BF16), vm(flat, F32), vm((pixels, 128), F32),
        vm(flat, BF16), vm(flat, BF16), vm(flat, F32),
        vm(flat, BF16), vm(flat, BF16), vm(flat, BF16), vm(flat, BF16),
        *[vm(shape, BF16) for shapes in hold for shape in shapes],
        dma((4, 2)), dma((4, 2)),
        dma((views,)), dma((views,)), dma((views,)), dma((views,)), dma((views,)), dma((views,)),
        dma((total,)), dma((total,)), dma((total, strips)), dma((total, strips)),
        dma((total, zs)), dma((total, zs)), dma((total, strips)), dma((total, strips)),
    ]
    spec = pl.BlockSpec(memory_space=pltpu.VMEM)
    stay = pl.BlockSpec(memory_space=pl.ANY)
    kind = BF16 if exact else F32
    conv_s = (2, cut, chan)
    attn_s = (4, slab, chan)
    outs = pl.pallas_call(
        functools.partial(kernel, (views, strips, rows, width, chan)),
        out_shape=(
            jax.ShapeDtypeStruct(flat, BF16),
            jax.ShapeDtypeStruct(conv_s, kind),
            jax.ShapeDtypeStruct(attn_s, kind),
        ),
        in_specs=[spec] * 2 + [stay] * 6,
        out_specs=(spec, spec, spec),
        scratch_shapes=scratch,
        compiler_params=pltpu.CompilerParams(
            collective_id=0, has_side_effects=True, vmem_limit_bytes=56 * 1024 * 1024
        ),
    )(
        features.reshape(flat),
        cotangent.reshape(flat),
        conv_first.reshape(3, 3 * chan, chan),
        conv_second.reshape(3, 3 * chan, chan),
        w_query, w_key, w_value, w_out,
    )
    outs = pl.pallas_call(
        widen,
        out_shape=(
            jax.ShapeDtypeStruct(flat, BF16),
            jax.ShapeDtypeStruct(conv_s, F32),
            jax.ShapeDtypeStruct(attn_s, F32),
        ),
        in_specs=[spec] * 3,
        out_specs=(spec, spec, spec),
    )(*outs)
    return (outs[0].reshape(features.shape), outs[1], outs[2])


def solution(mesh):
    rows = P(("orbit", "view"), "strip", None, None)
    grads = P("orbit", "view", None)
    return jax.shard_map(
        body,
        mesh=mesh,
        in_specs=(rows, rows, P(), P(), P(), P(), P(), P()),
        out_specs=(rows, grads, grads),
        check_vma=False,
    )
```

```python
import functools

import jax
import jax.numpy as jnp
from jax import lax
from jax.experimental import pallas as pl
from jax.experimental.pallas import tpu as pltpu
from jax.sharding import PartitionSpec as P

MESH = pl.DeviceIdType.MESH
F32 = jnp.float32
BF16 = jnp.bfloat16
NT = (((1,), (1,)), ((), ()))
TN = (((0,), (0,)), ((), ()))


def dot(a, b):
    return jnp.dot(a, b, preferred_element_type=F32)


def dot_nt(a, b):
    return lax.dot_general(a, b, NT, preferred_element_type=F32)


def dot_tn(a, b):
    return lax.dot_general(a, b, TN, preferred_element_type=F32)


def silu(x):
    return x * jax.nn.sigmoid(x)


def silu_slope(x):
    sigma = jax.nn.sigmoid(x)
    return sigma * (1.0 + x * (1.0 - sigma))


def kernel(
    dims, feat, cot, w1h, w2h, wqh, wkh, wvh, woh, gfeat, conv_out, attn_out,
    w1, w2, wq, wk, wv, wo, load,
    cols1, cols2, colsg, halo, hidden, normed, normed_f, inv, g2, gs,
    normp, cotp, backp, gn,
    part_a, part_b, part_c, r1a, r1b, r1c, t1a, t1b, t1c, r2a, r2b, r2c,
    t2a, t2b, t2c, r3a, r3b, r3c, r4a, r4b, r4c,
    halo_send, halo_recv, cot_send, cot_recv, nrm_send, nrm_recv, bck_send, bck_recv,
    s1_send, s1_recv, s2_send, s2_recv, s3_send, s3_recv, s4_send, s4_recv,
):
    views, strips, rows, width, chan = dims
    pixels = rows * width
    share = pixels // views
    zs = views // 2
    view = lax.axis_index("view")
    strip = lax.axis_index("strip")
    core = lax.rem(view, 2)
    zed = lax.div(view, 2)

    loads = [
        pltpu.make_async_copy(src, dst, load.at[i])
        for i, (src, dst) in enumerate(
            ((w1h, w1), (w2h, w2), (woh, wo), (wqh, wq), (wkh, wk), (wvh, wv))
        )
    ]
    for item in loads:
        item.start()
    barrier = pltpu.get_barrier_semaphore()
    for k in range(1, views):
        pl.semaphore_signal(
            barrier, inc=1, device_id={"view": lax.rem(view + k, views)}, device_id_type=MESH
        )
    for k in range(1, strips):
        pl.semaphore_signal(
            barrier, inc=1, device_id={"strip": lax.rem(strip + k, strips)}, device_id_type=MESH
        )

    @pl.when(strip == 0)
    def _():
        for e in range(2):
            halo[e, 0] = jnp.zeros((2 * width, chan), BF16)

    @pl.when(strip == strips - 1)
    def _():
        for e in range(2):
            halo[e, 1] = jnp.zeros((2 * width, chan), BF16)

    pl.semaphore_wait(barrier, views - 1 + strips - 1)

    def halo_copies(e, ref):
        up = pltpu.make_async_remote_copy(
            src_ref=ref.at[pl.ds(0, 2 * width)], dst_ref=halo.at[e, 1],
            send_sem=halo_send.at[e, 0], recv_sem=halo_recv.at[e, 0],
            device_id={"strip": lax.max(strip - 1, 0)}, device_id_type=MESH,
        )
        down = pltpu.make_async_remote_copy(
            src_ref=ref.at[pl.ds(pixels - 2 * width, 2 * width)], dst_ref=halo.at[e, 0],
            send_sem=halo_send.at[e, 1], recv_sem=halo_recv.at[e, 1],
            device_id={"strip": lax.min(strip + 1, strips - 1)}, device_id_type=MESH,
        )
        return up, down

    def halo_start(e, ref):
        up, down = halo_copies(e, ref)
        pl.when(strip > 0)(up.start)
        pl.when(strip < strips - 1)(down.start)

    def halo_wait(e, ref):
        up, down = halo_copies(e, ref)

        @pl.when(strip > 0)
        def _():
            up.wait_send()
            down.wait_recv()

        @pl.when(strip < strips - 1)
        def _():
            down.wait_send()
            up.wait_recv()

    def spread(src, dst, send, recv):
        out = []
        for k in range(1, views):
            peer = lax.rem(view + k, views)
            out.append(
                pltpu.make_async_remote_copy(
                    src_ref=src.at[pl.ds(pl.multiple_of(peer * share, share), share)],
                    dst_ref=dst.at[pl.ds(pl.multiple_of(view * share, share), share)],
                    send_sem=send.at[k], recv_sem=recv.at[k],
                    device_id={"view": peer}, device_id_type=MESH,
                )
            )
        return out

    mine = pl.ds(pl.multiple_of(view * share, share), share)

    def start(copies):
        for copy in copies:
            copy.start()

    def wait(copies):
        for copy in copies:
            copy.wait()

    wide = pixels + 2 * width
    place = lax.broadcasted_iota(jnp.int32, (wide, chan), 0)
    above = jnp.where(strip == 0, width, 0)
    below = jnp.where(strip == strips - 1, wide - width, wide)
    inside = (place >= above) & (place < below)

    def extend(e, centre):
        return jnp.concatenate(
            [halo[e, 0].astype(F32), centre.astype(F32), halo[e, 1].astype(F32)], axis=0
        )

    def build(cols, x):
        count = x.shape[0]
        column = lax.rem(lax.broadcasted_iota(jnp.int32, x.shape, 0), width)
        left = jnp.where(column == 0, 0.0, pltpu.roll(x, 1, 0))
        right = jnp.where(column == width - 1, 0.0, pltpu.roll(x, count - 1, 0))
        span = pl.ds(0, count)
        cols[span, pl.ds(0, chan)] = left.astype(BF16)
        cols[span, pl.ds(chan, chan)] = x.astype(BF16)
        cols[span, pl.ds(2 * chan, chan)] = right.astype(BF16)

    def conv(cols, w, count):
        total = None
        for r in range(3):
            term = dot(cols[pl.ds(r * width, count), :], w[r])
            total = term if total is None else total + term
        return total

    def conv_flip(cols, w, count):
        total = None
        for r in range(3):
            for s in range(3):
                term = dot_nt(
                    cols[pl.ds(r * width, count), pl.ds(s * chan, chan)],
                    w[2 - r, pl.ds((2 - s) * chan, chan), :],
                )
                total = term if total is None else total + term
        return total

    def wgrad(cols, d, out, skip):
        pieces, _, _, parts, unit, _ = out.shape
        per = 3 * chan // unit
        for r in range(3):
            value = dot_tn(cols[pl.ds(skip + r * width, pixels), :], d).astype(BF16)
            for m in range(per):
                u = r * per + m
                v, rest = divmod(u, pieces * parts)
                p, t = divmod(rest, parts)
                out[p, v // 2, v % 2, t] = value[m * unit : (m + 1) * unit]

    def group(base, part, r1, t1, r2, t2, r3, r4):
        parts = part.shape[3]

        def stage1(p):
            return [
                pltpu.make_async_remote_copy(
                    src_ref=part.at[p, :, 1 - core], dst_ref=r1.at[p],
                    send_sem=s1_send.at[base + p], recv_sem=s1_recv.at[base + p],
                    device_id={"view": view + 1 - 2 * core}, device_id_type=MESH,
                )
            ]

        def reduce1(p):
            for j in range(zs):
                for t in range(parts):
                    t1[p, t, j] = (
                        part[p, j, core, t].astype(F32) + r1[p, j, t].astype(F32)
                    ).astype(BF16)

        def stage2(p):
            out = []
            for k in range(1, parts):
                other = lax.rem(strip + k, strips)
                out.append(
                    pltpu.make_async_remote_copy(
                        src_ref=t1.at[p, other], dst_ref=r2.at[p, k - 1],
                        send_sem=s2_send.at[base + p, k], recv_sem=s2_recv.at[base + p, k],
                        device_id={"strip": other}, device_id_type=MESH,
                    )
                )
            return out

        def reduce2(p):
            own = strip if parts > 1 else 0
            for j in range(zs):
                value = t1[p, own, j].astype(F32)
                for k in range(1, parts):
                    value = value + r2[p, k - 1, j].astype(F32)
                t2[p, j] = value.astype(BF16)

        def stage3(p):
            out = []
            for k in range(1, zs):
                other = lax.rem(zed + k, zs)
                out.append(
                    pltpu.make_async_remote_copy(
                        src_ref=t2.at[p, other], dst_ref=r3.at[p, k - 1],
                        send_sem=s3_send.at[base + p, k], recv_sem=s3_recv.at[base + p, k],
                        device_id={"view": other * 2 + core}, device_id_type=MESH,
                    )
                )
            return out

        def reduce3(p):
            value = t2[p, zed].astype(F32)
            for k in range(1, zs):
                value = value + r3[p, k - 1].astype(F32)
            r4[p, strip] = value.astype(BF16)

        def stage4(p):
            out = []
            for k in range(1, strips):
                out.append(
                    pltpu.make_async_remote_copy(
                        src_ref=r4.at[p, strip], dst_ref=r4.at[p, strip],
                        send_sem=s4_send.at[base + p, k], recv_sem=s4_recv.at[base + p, k],
                        device_id={"strip": lax.rem(strip + k, strips)}, device_id_type=MESH,
                    )
                )
            return out

        def final(p):
            if parts > 1:
                return [r4[p, t].astype(F32) for t in range(parts)]
            value = r4[p, 0].astype(F32)
            for t in range(1, strips):
                value = value + r4[p, t].astype(F32)
            return [value]

        reduces = (None, reduce1, reduce2, reduce3)
        stages = (stage1, stage2, stage3, stage4)

        def launch():
            for p in range(part.shape[0]):
                start(stage1(p))

        def advance(k, p):
            wait(stages[k - 1](p))
            reduces[k](p)
            start(stages[k](p))

        def advance_all(k):
            for p in range(part.shape[0]):
                advance(k, p)

        def finish(store):
            for p in range(part.shape[0]):
                wait(stage4(p))
                for t, value in enumerate(final(p)):
                    store(p * parts + t, value)

        return launch, advance_all, finish

    count_a = part_a.shape[0]
    count_b = part_b.shape[0]
    launch_a, step_a, finish_a = group(0, part_a, r1a, t1a, r2a, t2a, r3a, r4a)
    launch_b, step_b, finish_b = group(count_a, part_b, r1b, t1b, r2b, t2b, r3b, r4b)
    launch_c, step_c, finish_c = group(count_a + count_b, part_c, r1c, t1c, r2c, t2c, r3c, r4c)

    halo_start(0, feat)
    cot_copies = spread(cot, cotp, cot_send, cot_recv)
    start(cot_copies)
    cotp[mine, :] = cot[mine, :]
    halo_wait(0, feat)
    build(cols1, silu(extend(0, feat[...])))
    loads[0].wait()
    hidden[...] = conv(cols1, w1, wide).astype(BF16)
    act2 = silu(hidden[...].astype(F32)).astype(BF16).astype(F32)
    build(cols2, jnp.where(inside, act2, 0.0))
    loads[1].wait()
    summed = (feat[...].astype(F32) + conv(cols2, w2, pixels)).astype(BF16).astype(F32)
    centred = summed - jnp.mean(summed, axis=-1, keepdims=True)
    scale = lax.rsqrt(jnp.mean(centred * centred, axis=-1, keepdims=True) + 1e-05)
    inv[...] = jnp.broadcast_to(scale, inv.shape)
    nf = centred * scale
    normed_f[...] = nf
    normed[...] = nf.astype(BF16)
    nrm_copies = spread(normed, normp, nrm_send, nrm_recv)
    start(nrm_copies)
    normp[mine, :] = normed[mine, :]
    wait(cot_copies)
    loads[2].wait()
    gmix = dot_nt(cotp[...], wo[...]).astype(BF16)
    for item in loads[3:]:
        item.wait()
    wait(nrm_copies)

    rp = normp[...]
    query = dot(rp, wq[...]).astype(BF16)
    key = dot(rp, wk[...]).astype(BF16)
    value = dot(rp, wv[...]).astype(BF16)
    n = views * share
    ia = lax.rem(lax.broadcasted_iota(jnp.int32, (n, n), 0), share)
    ib = lax.rem(lax.broadcasted_iota(jnp.int32, (n, n), 1), share)
    factor = chan ** (-0.5)
    scores = jnp.where(ia == ib, dot_nt(query, key) * factor, -jnp.inf)
    expo = jnp.exp(scores - jnp.max(scores, axis=-1, keepdims=True))
    prob_f = expo / jnp.sum(expo, axis=-1, keepdims=True)
    prob = prob_f.astype(BF16)
    mixed = dot(prob, value).astype(BF16)
    grad_prob = dot_nt(gmix, value)
    weighted = prob_f * grad_prob
    inner = jnp.sum(weighted, axis=-1, keepdims=True)
    grad_score = (prob_f * (grad_prob - inner) * factor).astype(BF16)
    grad_value = dot_tn(prob, gmix).astype(BF16)
    grad_query = dot(grad_score, key).astype(BF16)
    grad_key = dot_tn(grad_score, query).astype(BF16)
    back = dot_nt(grad_query, wq[...]) + dot_nt(grad_key, wk[...]) + dot_nt(grad_value, wv[...])
    backp[...] = back.astype(BF16)
    bck_copies = spread(backp, gn, bck_send, bck_recv)
    start(bck_copies)
    gn[mine, :] = backp[mine, :]
    parts = part_a.shape[3]
    unit = chan // (views * parts)
    for t, (lhs, rhs) in enumerate(
        ((rp, grad_query), (rp, grad_key), (rp, grad_value), (mixed, cotp[...]))
    ):
        term = dot_tn(lhs, rhs).astype(BF16)
        for u in range(views * parts):
            v, q = divmod(u, parts)
            part_a[0, v // 2, v % 2, q, t] = term[u * unit : (u + 1) * unit]
    launch_a()
    step_a(1)

    wait(bck_copies)
    gnf = gn[...].astype(F32)
    nf = normed_f[...]
    gsum = cot[...].astype(F32) + inv[:, 0:1] * (
        gnf
        - jnp.mean(gnf, axis=-1, keepdims=True)
        - nf * jnp.mean(gnf * nf, axis=-1, keepdims=True)
    )
    gs[...] = gsum
    g2[...] = gsum.astype(BF16)
    halo_start(1, g2)
    wgrad(cols2, g2[...], part_b, 0)
    launch_b()
    step_a(2)
    step_b(1)
    halo_wait(1, g2)
    build(colsg, extend(1, g2[...]))
    slope = conv_flip(colsg, w2, wide)
    g1 = (slope * silu_slope(hidden[...].astype(F32))).astype(BF16)
    wgrad(cols1, g1[width : width + pixels], part_c, width)
    launch_c()
    build(colsg, jnp.where(inside, g1.astype(F32), 0.0))
    step_c(1)
    step_b(2)
    slope = conv_flip(colsg, w1, pixels)
    gfeat[...] = (gs[...] + slope * silu_slope(feat[...].astype(F32))).astype(BF16)
    step_a(3)
    step_c(2)
    step_b(3)
    step_c(3)

    def store_a(u, value):
        attn_out[:, pl.ds(u * unit, unit), :] = value.astype(attn_out.dtype)

    def store_conv(i):
        def store(u, value):
            size = value.shape[0]
            conv_out[i, pl.ds(u * size, size), :] = value.astype(conv_out.dtype)

        return store

    finish_a(store_a)
    finish_b(store_conv(1))
    finish_c(store_conv(0))


def widen(a, b, c, x, y, z):
    x[...] = a[...]
    y[...] = b[...].astype(F32)
    z[...] = c[...].astype(F32)


def body(features, cotangent, conv_first, conv_second, w_query, w_key, w_value, w_out):
    views = lax.axis_size("view")
    strips = lax.axis_size("strip")
    _, rows, width, chan = features.shape
    pixels = rows * width
    zs = views // 2
    cut = 9 * chan // views
    slab = chan // views
    vm = pltpu.VMEM
    dma = pltpu.SemaphoreType.DMA
    padded = pixels + 2 * width
    far = pixels + 4 * width
    flat = (pixels, chan)
    exact = cut % (16 * strips) == 0 and slab % (16 * strips) == 0
    parts = strips if exact else 1
    pieces = 3 if cut % (48 * parts) == 0 else 1
    conv_u = (cut // (parts * pieces), chan)
    attn_u = (4, slab // parts, chan)
    units = ((1, attn_u), (pieces, conv_u), (pieces, conv_u))
    total = 1 + 2 * pieces
    hold = [
        [(n, zs, 2, parts) + u for n, u in units],
        [(n, zs, parts) + u for n, u in units],
        [(n, parts, zs) + u for n, u in units],
        [(n, max(parts - 1, 1), zs) + u for n, u in units],
        [(n, zs) + u for n, u in units],
        [(n, zs - 1) + u for n, u in units],
        [(n, strips) + u for n, u in units],
    ]
    conv_k = (3, 3 * chan, chan)
    square = (chan, chan)
    scratch = [
        vm(conv_k, BF16), vm(conv_k, BF16),
        vm(square, BF16), vm(square, BF16), vm(square, BF16), vm(square, BF16), dma((6,)),
        vm((far, 3 * chan), BF16), vm((padded, 3 * chan), BF16), vm((far, 3 * chan), BF16),
        vm((2, 2, 2 * width, chan), BF16), vm((padded, chan), BF16),
        vm(flat, BF16), vm(flat, F32), vm((pixels, 128), F32), vm(flat, BF16), vm(flat, F32),
        vm(flat, BF16), vm(flat, BF16), vm(flat, BF16), vm(flat, BF16),
        *[vm(shape, BF16) for shapes in hold for shape in shapes],
        dma((2, 2)), dma((2, 2)),
        dma((views,)), dma((views,)), dma((views,)), dma((views,)), dma((views,)), dma((views,)),
        dma((total,)), dma((total,)), dma((total, strips)), dma((total, strips)),
        dma((total, zs)), dma((total, zs)), dma((total, strips)), dma((total, strips)),
    ]
    spec = pl.BlockSpec(memory_space=pltpu.VMEM)
    stay = pl.BlockSpec(memory_space=pl.ANY)
    kind = BF16 if exact else F32
    conv_s = (2, cut, chan)
    attn_s = (4, slab, chan)
    outs = pl.pallas_call(
        functools.partial(kernel, (views, strips, rows, width, chan)),
        out_shape=(
            jax.ShapeDtypeStruct(flat, BF16),
            jax.ShapeDtypeStruct(conv_s, kind),
            jax.ShapeDtypeStruct(attn_s, kind),
        ),
        in_specs=[spec] * 2 + [stay] * 6,
        out_specs=(spec, spec, spec),
        scratch_shapes=scratch,
        compiler_params=pltpu.CompilerParams(
            collective_id=0, has_side_effects=True, vmem_limit_bytes=56 * 1024 * 1024
        ),
    )(
        features.reshape(flat),
        cotangent.reshape(flat),
        conv_first.reshape(3, 3 * chan, chan),
        conv_second.reshape(3, 3 * chan, chan),
        w_query, w_key, w_value, w_out,
    )
    outs = pl.pallas_call(
        widen,
        out_shape=(
            jax.ShapeDtypeStruct(flat, BF16),
            jax.ShapeDtypeStruct(conv_s, F32),
            jax.ShapeDtypeStruct(attn_s, F32),
        ),
        in_specs=[spec] * 3,
        out_specs=(spec, spec, spec),
    )(*outs)
    return (outs[0].reshape(features.shape), outs[1], outs[2])


def solution(mesh):
    rows = P(("orbit", "view"), "strip", None, None)
    grads = P("orbit", "view", None)
    return jax.shard_map(
        body,
        mesh=mesh,
        in_specs=(rows, rows, P(), P(), P(), P(), P(), P()),
        out_specs=(rows, grads, grads),
        check_vma=False,
    )
```
